256 devices in a mesh: head: 8 (over x, core), seq: 32 (over z, y).
Axes of the slice: x: 4, y: 4, z: 8, core: 2. Of those that a mesh axis runs over, the one named last changes fastest.
Arguments:
- queries: bfloat16 [16384, 128, 128], P(('seq', 'head')), may hold values from -12 to 12
- keys: bfloat16 [16384, 8, 128], P(('seq', 'head')), may hold values from -7.5 to 7.5
- values: bfloat16 [16384, 8, 128], P(('seq', 'head')), may hold values from -6 to 6
- doc_ids: int32 [16384], replicated, may hold values from 0 to 31, never falling along the last dimension, each value on 1 to 2048 neighbouring positions
Outputs:
- attn_out: bfloat16 [16384, 128, 128], P('seq', 'head')
The draws below stay inside these ranges and needn't reach their ends.
Inputs may be any that keep to these rules, and one draw needn't show every extreme that they name: `doc_ids`: document numbers never fall along the sequence; every document holds 1 to 2048 tokens and one holds exactly 2048.
All inputs are finite; a program needn't handle non-finite values.
Results may differ from the reference program's by a relative error of at most 0.0031.
Values may be sent and summed in bfloat16 or wider, within the bound.
A program may use at most 64 MiB of HBM per device.

```python
import math
import jax
import jax.numpy as jnp
import numpy as np
from jax import lax

DH = 128
QH = 128
KVH = 8
SEQ_DEV = 512
MAXDOC = 2048
TOKENS = 16384
N_SEQ = 32


def draw_queries(key, part):
    base = 2.0 * jax.random.normal(jax.random.fold_in(key, 1), (TOKENS, QH, DH), jnp.float32)
    base = jnp.clip(base, -12.0, 12.0)
    return base.astype(jnp.bfloat16)


def draw_keys(key, part):
    base = jax.random.normal(jax.random.fold_in(key, 2), (TOKENS, KVH, DH), jnp.float32)
    base = jnp.clip(base, -6.0, 6.0)
    return base.astype(jnp.bfloat16)


def shard_levels(own_key, extent, cuts, least, high):
    def one(dim, blocks):
        heights = jax.random.uniform(jax.random.fold_in(jax.random.fold_in(own_key, 6), dim), (blocks,), jnp.float32, least / len(cuts), high / len(cuts))
        return jnp.repeat(jnp.exp(heights), extent[dim] // blocks).reshape((-1,) + (1,) * (len(extent) - dim - 1))

    factor_of = one(*cuts[0])
    for cut in cuts[1:]:
        factor_of = factor_of * one(*cut)
    return factor_of


def profile(amount, total, limit, lean):
    loads = [(1 << 20) // math.isqrt(grade ** lean) + 1 for grade in range(2, amount + 1)]
    rest, counts = total - limit - (amount - 1), [1] * (amount - 1)
    while rest > 0:
        candidates = [i for i in range(amount - 1) if counts[i] < limit]
        pool, budget = sum([loads[i] for i in candidates]), rest
        for i in candidates:
            addition = min(limit - counts[i], max(1, budget * loads[i] // pool), rest)
            counts[i] = counts[i] + addition
            rest = rest - addition
    return np.array([limit] + counts)


def ragged_sizes(rng, amount, total, bound, slope):
    if amount == 2:
        one = jax.random.randint(rng, (), max(1, total - bound), min(bound, total - 1) + 1)
        return jnp.stack([one, total - one])
    lengths = jnp.asarray(profile(amount, total, bound, slope), jnp.int32)
    twos = (amount - 1) // 2
    source_of, receiver = lengths[1:1 + 2 * twos:2], lengths[2:2 + 2 * twos:2]
    margin = jnp.minimum(source_of - 1, bound - receiver)
    passed = jax.random.randint(jax.random.fold_in(rng, 1), (twos,), 0, 1 << 20) % (margin + 1)
    lengths = lengths.at[1:1 + 2 * twos:2].set(source_of - passed).at[2:2 + 2 * twos:2].set(receiver + passed)
    return lengths[jax.random.permutation(jax.random.fold_in(rng, 2), amount)]


def gaussian(key, shape, spread, reach, cuts=(), kind=jnp.bfloat16):
    level = shard_levels(key, shape, cuts, -0.22, 0.18) if cuts else 1.0
    values = jax.random.normal(key, shape, jnp.float32) * spread * level
    return jnp.minimum(jnp.maximum(values, -reach), reach).astype(kind)


def setup_inputs(seed: int = 0) -> dict:
    arg_keys = jax.random.split(jax.random.key(seed), 5)
    queries = draw_queries(jax.random.fold_in(arg_keys[4], 71), 0)
    keys = draw_keys(jax.random.fold_in(arg_keys[4], 71), 0)
    values = gaussian(arg_keys[2], (TOKENS, KVH, DH), 1.0, 6.0, ((0, 256),))
    doc_ids = jnp.searchsorted(jnp.cumsum(ragged_sizes(arg_keys[3], N_SEQ, TOKENS, MAXDOC, 2)), jnp.arange(TOKENS), side="right").astype(jnp.int32)
    return dict(queries=queries, keys=keys, values=values, doc_ids=doc_ids)


def reference(queries, keys, values, doc_ids):
    head_width = queries.shape[2]
    kv_groups = keys.shape[1]
    per_group = queries.shape[1] // kv_groups
    window = MAXDOC + SEQ_DEV
    blocks = TOKENS // SEQ_DEV
    score_scale = 1.0 / math.sqrt(head_width)
    grouped_q = queries.reshape(TOKENS, kv_groups, per_group, head_width)
    zero_index = jnp.zeros((), jnp.int32)

    def one_block(index):
        block = index // kv_groups
        group = index % kv_groups
        q_start = (block * SEQ_DEV).astype(jnp.int32)
        k_start = jnp.maximum(q_start + SEQ_DEV - window, 0).astype(jnp.int32)
        q_block = lax.dynamic_slice(grouped_q, (q_start, group, zero_index, zero_index), (SEQ_DEV, 1, per_group, head_width))[:, 0].astype(jnp.float32)
        k_block = lax.dynamic_slice(keys, (k_start, group, zero_index), (window, 1, head_width))[:, 0].astype(jnp.float32)
        v_block = lax.dynamic_slice(values, (k_start, group, zero_index), (window, 1, head_width))[:, 0].astype(jnp.float32)
        q_pos = q_start + jnp.arange(SEQ_DEV, dtype=jnp.int32)
        k_pos = k_start + jnp.arange(window, dtype=jnp.int32)
        q_doc = lax.dynamic_slice_in_dim(doc_ids, q_start, SEQ_DEV)
        k_doc = lax.dynamic_slice_in_dim(doc_ids, k_start, window)
        allowed = (q_doc[:, None] == k_doc[None, :]) & (k_pos[None, :] <= q_pos[:, None])
        allowed_b = allowed[:, None, :]
        scores = jnp.einsum('thd,sd->ths', q_block, k_block) * score_scale
        masked = jnp.where(allowed_b, scores, -1e+30)
        top_score = lax.optimization_barrier(jnp.max(masked, axis=-1))
        weights = jnp.where(allowed_b, jnp.exp(masked - top_score[..., None]), 0.0)
        total = lax.optimization_barrier(jnp.sum(weights, axis=-1))
        rounded = lax.optimization_barrier(weights.astype(jnp.bfloat16)).astype(jnp.float32)
        mixed = jnp.einsum('ths,sd->thd', rounded, v_block) / total[..., None]
        return mixed.astype(jnp.bfloat16)
    result = lax.map(one_block, jnp.arange(blocks * kv_groups, dtype=jnp.int32))
    result = result.reshape(blocks, kv_groups, SEQ_DEV, per_group, head_width)
    result = result.transpose(0, 2, 1, 3, 4).reshape(TOKENS, kv_groups * per_group, head_width)
    return result
```

```python
import functools
import math

import jax
import jax.numpy as jnp
from jax import lax
from jax.experimental import pallas as pl
from jax.experimental.pallas import tpu as pltpu
from jax.sharding import PartitionSpec as P

MESH = pl.DeviceIdType.MESH
REACH = 4
BLOCK = 512
PIECE = 64
CHUNK = 128
HEADS = 16
WIDTH = 128
WINDOW = REACH * BLOCK + CHUNK
TILE = 32
ROWS = TILE * HEADS
DOCS = 32
PENALTY = 32768.0
SCALE = math.log2(math.e) / math.sqrt(WIDTH)
PEERS = [(0, 1), (1, 0), (1, 1), (3, 0), (3, 1), (2, 0), (2, 1)]


def kernel(q_hbm, kv_hbm, doc_ref, out_hbm, kv, qb, ab, tab, sb, ob,
           kv_send, kv_recv, q_send, q_recv, seq_send, seq_recv, loc_sem, out_sem):
    head, seq = lax.axis_index("head"), lax.axis_index("seq")
    x, core = head // 2, head % 2

    def to(dx, dc):
        return 2 * ((x + dx) % 4) + (core + dc) % 2

    def came(dx, dc):
        return 2 * ((x - dx + 4) % 4) + (core + dc) % 2

    barrier = pltpu.get_barrier_semaphore()
    for dx, dc in PEERS:
        pl.semaphore_signal(barrier, inc=1, device_id={"head": to(dx, dc)}, device_id_type=MESH)
    for d in range(1, REACH + 1):
        pl.semaphore_signal(barrier, inc=1, device_id={"seq": (seq + 32 - d) % 32}, device_id_type=MESH)

    own_rows = pl.ds(pl.multiple_of(REACH * BLOCK + PIECE * head, PIECE), PIECE)
    own_kv = pltpu.make_async_copy(kv_hbm.at[head], kv.at[own_rows, 128:384], loc_sem.at[0])
    own_kv.start()
    own_q = pltpu.make_async_copy(
        q_hbm.at[:, pl.ds(pl.multiple_of(HEADS * head, HEADS), HEADS), :],
        qb.at[pl.ds(pl.multiple_of(PIECE * head, PIECE), PIECE)], loc_sem.at[1])
    own_q.start()
    pl.semaphore_wait(barrier, len(PEERS) + REACH)

    def kv_copy(dx, dc, sender):
        target = to(dx, dc)
        rows = pl.ds(pl.multiple_of(REACH * BLOCK + PIECE * sender, PIECE), PIECE)
        return pltpu.make_async_remote_copy(
            kv_hbm.at[target], kv.at[rows, 128:384],
            kv_send.at[2 * dx + dc], kv_recv.at[2 * dx + dc],
            device_id={"head": target}, device_id_type=MESH)

    def q_copy(dx, dc, sender):
        target = to(dx, dc)
        return pltpu.make_async_remote_copy(
            q_hbm.at[:, pl.ds(pl.multiple_of(HEADS * target, HEADS), HEADS), :],
            qb.at[pl.ds(pl.multiple_of(PIECE * sender, PIECE), PIECE)],
            q_send.at[2 * dx + dc], q_recv.at[2 * dx + dc],
            device_id={"head": target}, device_id_type=MESH)

    def seq_copy(d):
        return pltpu.make_async_remote_copy(
            kv.at[REACH * BLOCK:, 128:384],
            kv.at[(REACH - d) * BLOCK:(REACH - d + 1) * BLOCK, 128:384],
            seq_send.at[d - 1], seq_recv.at[d - 1],
            device_id={"seq": (seq + d) % 32}, device_id_type=MESH)

    for dx, dc in PEERS:
        kv_copy(dx, dc, head).start()
    for dx, dc in PEERS:
        q_copy(dx, dc, head).start()

    own_kv.wait()
    for dx, dc in PEERS:
        kv_copy(dx, dc, came(dx, dc)).wait_recv()
    for d in range(1, REACH + 1):
        seq_copy(d).start()

    lane = lax.broadcasted_iota(jnp.int32, (BLOCK, 128), 1)
    for b in range(REACH + 1):
        row = doc_ref[pl.ds((seq + 32 - REACH + b) % 32, 1), :]
        cols = jnp.broadcast_to(row, (128, BLOCK)).astype(jnp.float32).T.astype(jnp.int32)
        same = cols == lane
        kv[b * BLOCK:(b + 1) * BLOCK, 0:128] = jnp.where(same, 1.0, 0.0).astype(jnp.bfloat16)
        kv[b * BLOCK:(b + 1) * BLOCK, 384:512] = jnp.ones((BLOCK, 128), jnp.bfloat16)
        if b == REACH:
            tab[...] = jnp.where(same | (lane >= DOCS), 0.0, -PENALTY)

    def spread(i, _):
        rows = pl.ds(pl.multiple_of(16 * i, 16), 16)
        ab[rows] = jnp.broadcast_to(tab[rows, :][:, None, :], (16, HEADS, 128)).astype(jnp.bfloat16)
        return 0

    lax.fori_loop(0, BLOCK // 16, spread, 0)

    own_q.wait()
    q_copy(0, 1, came(0, 1)).wait_recv()
    for d in range(1, REACH + 1):
        seq_copy(d).wait_recv()

    tiles = CHUNK // TILE
    steps = 4 * tiles

    def place(t):
        order = t // tiles
        dx = order + jnp.where(order == 2, 1, 0) - jnp.where(order == 3, 1, 0)
        chunk = (x - dx + 4) % 4
        return chunk, dx, t % tiles

    def scores(t, slot):
        chunk, _, part = place(t)
        rows = pl.ds(pl.multiple_of(CHUNK * chunk + TILE * part, TILE), TILE)
        left = jnp.concatenate(
            [ab[rows].reshape(ROWS, WIDTH), qb[rows].reshape(ROWS, WIDTH)], axis=1)
        keys = kv[pl.ds(pl.multiple_of(CHUNK * chunk, CHUNK), WINDOW), 0:256]
        sb[slot] = lax.dot_general(
            left, keys, (((1,), (1,)), ((), ())), preferred_element_type=jnp.float32)

    def weigh(t, slot):
        chunk, _, part = place(t)
        token = lax.broadcasted_iota(jnp.int32, (ROWS, CHUNK), 0) // HEADS + TILE * part
        key = lax.broadcasted_iota(jnp.int32, (ROWS, CHUNK), 1)
        last = jnp.where(key <= token, sb[slot, :, WINDOW - CHUNK:], -PENALTY)
        s = jnp.concatenate([sb[slot, :, :WINDOW - CHUNK], last], axis=1)
        top = jnp.max(s, axis=1, keepdims=True)
        weights = jnp.exp2((s - top) * SCALE).astype(jnp.bfloat16)
        vals = kv[pl.ds(pl.multiple_of(CHUNK * chunk, CHUNK), WINDOW), 256:512]
        o = jnp.dot(weights, vals, preferred_element_type=jnp.float32)
        rows = pl.ds(pl.multiple_of(CHUNK * chunk + TILE * part, TILE), TILE)
        ob[rows] = (o[:, :128] / o[:, 128:]).astype(jnp.bfloat16).reshape(TILE, HEADS, WIDTH)

    def pair(j, _):
        t = 2 * j
        scores(t + 1, 1)
        weigh(t, 0)
        following = jnp.minimum(t + 2, steps - 1)

        @pl.when((following % tiles == 0) & (t + 2 < steps))
        def _():
            _, dx, _ = place(following)
            for dc in range(2):
                source = 2 * ((x - dx + 4) % 4) + (core + dc) % 2
                pltpu.make_async_remote_copy(
                    q_hbm.at[:, 0:HEADS, :],
                    qb.at[pl.ds(pl.multiple_of(PIECE * source, PIECE), PIECE)],
                    q_send.at[0], q_recv.at[2 * dx + dc],
                    device_id={"head": source}, device_id_type=MESH).wait_recv()

        scores(following, 0)
        weigh(t + 1, 1)
        return 0

    scores(jnp.int32(0), 0)
    lax.fori_loop(0, steps // 2, pair, 0)
    out = pltpu.make_async_copy(ob, out_hbm, out_sem)
    out.start()
    for dx, dc in PEERS:
        kv_copy(dx, dc, head).wait_send()
        q_copy(dx, dc, head).wait_send()
    for d in range(1, REACH + 1):
        seq_copy(d).wait_send()
    out.wait()


def per_device(queries, keys, values, doc_ids):
    kv = jnp.concatenate([keys, values], axis=-1).transpose(1, 0, 2)
    docs = doc_ids.reshape(32, BLOCK)
    hbm = pl.BlockSpec(memory_space=pl.ANY)
    dma = pltpu.SemaphoreType.DMA
    return pl.pallas_call(
        kernel,
        out_shape=jax.ShapeDtypeStruct((BLOCK, HEADS, WIDTH), jnp.bfloat16),
        in_specs=[hbm, hbm, pl.BlockSpec(memory_space=pltpu.VMEM)],
        out_specs=hbm,
        scratch_shapes=[
            pltpu.VMEM(((REACH + 1) * BLOCK, 512), jnp.bfloat16),
            pltpu.VMEM((BLOCK, HEADS, WIDTH), jnp.bfloat16),
            pltpu.VMEM((BLOCK, HEADS, WIDTH), jnp.bfloat16),
            pltpu.VMEM((BLOCK, 128), jnp.float32),
            pltpu.VMEM((2, ROWS, WINDOW), jnp.float32),
            pltpu.VMEM((BLOCK, HEADS, WIDTH), jnp.bfloat16),
            dma((8,)), dma((8,)), dma((8,)), dma((8,)), dma((4,)), dma((4,)), dma((2,)), dma,
        ],
        compiler_params=pltpu.CompilerParams(
            collective_id=0, has_side_effects=True, vmem_limit_bytes=56 << 20),
    )(queries, kv, docs)


def solution(mesh):
    spec = P(("seq", "head"), None, None)
    return jax.shard_map(
        per_device, mesh=mesh, in_specs=(spec, spec, spec, P()),
        out_specs=P("seq", "head", None), check_vma=False)
```

```python
import functools
import math

import jax
import jax.numpy as jnp
from jax import lax
from jax.experimental import pallas as pl
from jax.experimental.pallas import tpu as pltpu
from jax.sharding import PartitionSpec as P

MESH = pl.DeviceIdType.MESH
REACH = 4
BLOCK = 512
PIECE = 64
CHUNK = 128
HEADS = 16
WIDTH = 128
WINDOW = REACH * BLOCK + CHUNK
TILE = 32
ROWS = TILE * HEADS
DOCS = 32
PENALTY = 32768.0
SCALE = math.log2(math.e) / math.sqrt(WIDTH)
PEERS = [(0, 1), (1, 0), (1, 1), (3, 0), (3, 1), (2, 0), (2, 1)]


def kernel(q_hbm, k_hbm, v_hbm, doc_hbm, ob, kin, vin, kvs, docs, kv, qb, ab, tab, sb,
           kv_send, kv_recv, q_send, q_recv, seq_send, seq_recv, loc_sem, doc_sem):
    head, seq = lax.axis_index("head"), lax.axis_index("seq")
    x, core = head // 2, head % 2
    y = seq % 4

    def to(dx, dc):
        return 2 * ((x + dx) % 4) + (core + dc) % 2

    def came(dx, dc):
        return 2 * ((x - dx + 4) % 4) + (core + dc) % 2

    k_in = pltpu.make_async_copy(k_hbm, kin, loc_sem.at[2])
    v_in = pltpu.make_async_copy(v_hbm, vin, loc_sem.at[3])
    k_in.start()
    v_in.start()
    doc_in = []
    for b in range(REACH + 1):
        start = pl.multiple_of((seq + 32 - REACH + b) % 32 * BLOCK, BLOCK)
        doc_in.append(pltpu.make_async_copy(doc_hbm.at[pl.ds(start, BLOCK)], docs.at[b, 0], doc_sem.at[b]))
        doc_in[-1].start()
    own_q = pltpu.make_async_copy(
        q_hbm.at[:, pl.ds(pl.multiple_of(HEADS * head, HEADS), HEADS), :],
        qb.at[pl.ds(pl.multiple_of(PIECE * head, PIECE), PIECE)], loc_sem.at[1])
    own_q.start()

    barrier = pltpu.get_barrier_semaphore()
    for dx, dc in PEERS:
        pl.semaphore_signal(barrier, inc=1, device_id={"head": to(dx, dc)}, device_id_type=MESH)
    up = (seq // 4) * 4 + (y + 1) % 4
    down = (seq // 4) * 4 + (y + 3) % 4
    for other in (up, down, (seq + 28) % 32):
        pl.semaphore_signal(barrier, inc=1, device_id={"seq": other}, device_id_type=MESH)

    k_in.wait()
    v_in.wait()
    kvs[:, :, 0:128] = jnp.transpose(kin[...], (1, 0, 2))
    kvs[:, :, 128:256] = jnp.transpose(vin[...], (1, 0, 2))
    pl.semaphore_wait(barrier, len(PEERS) + 3)

    def kv_copy(dx, dc, sender):
        target = to(dx, dc)
        rows = pl.ds(pl.multiple_of(REACH * BLOCK + PIECE * sender, PIECE), PIECE)
        return pltpu.make_async_remote_copy(
            kvs.at[target], kv.at[rows, 128:384],
            kv_send.at[2 * dx + dc], kv_recv.at[2 * dx + dc],
            device_id={"head": target}, device_id_type=MESH)

    def q_copy(dx, dc, sender):
        target = to(dx, dc)
        return pltpu.make_async_remote_copy(
            q_hbm.at[:, pl.ds(pl.multiple_of(HEADS * target, HEADS), HEADS), :],
            qb.at[pl.ds(pl.multiple_of(PIECE * sender, PIECE), PIECE)],
            q_send.at[2 * dx + dc], q_recv.at[2 * dx + dc],
            device_id={"head": target}, device_id_type=MESH)

    own_rows = pl.ds(pl.multiple_of(REACH * BLOCK + PIECE * head, PIECE), PIECE)
    own_kv = pltpu.make_async_copy(kvs.at[head], kv.at[own_rows, 128:384], loc_sem.at[0])
    own_kv.start()
    for dx, dc in PEERS:
        kv_copy(dx, dc, head).start()
    for dx, dc in PEERS:
        q_copy(dx, dc, head).start()

    def part(d, dx):
        return pl.ds(pl.multiple_of(
            (REACH - d) * BLOCK + CHUNK * ((x - dx + 4) % 4), CHUNK), CHUNK)

    def pass_on(src, d, dx, target, lane):
        return pltpu.make_async_remote_copy(
            kv.at[part(src, dx), 128:384], kv.at[part(d, dx), 128:384],
            seq_send.at[4 * lane + dx], seq_recv.at[4 * (d - 1) + dx],
            device_id={"seq": target}, device_id_type=MESH)

    def arrive(d, dx):
        pass_on(d, d, dx, up, 0).wait_recv()

    def own_part(dx):
        if dx == 0:
            own_kv.wait()
        else:
            kv_copy(dx, 0, came(dx, 0)).wait_recv()
        kv_copy(dx, 1, came(dx, 1)).wait_recv()
        pass_on(0, 4, dx, (seq + 4) % 32, 0).start()

        @pl.when(y < 3)
        def _():
            pass_on(0, 1, dx, up, 1).start()

        @pl.when(y == 0)
        def _():
            pass_on(0, 3, dx, down, 2).start()

    def far_part(dx):
        arrive(4, dx)

        @pl.when(y > 0)
        def _():
            pass_on(4, 3, dx, down, 2).start()

        @pl.when(y == 3)
        def _():
            pass_on(4, 1, dx, up, 1).start()

    middle = (y == 1) | (y == 2)

    def near_part(dx):
        arrive(1, dx)

        @pl.when(middle)
        def _():
            pass_on(1, 2, dx, up, 3).start()

    def third_part(dx):
        arrive(3, dx)

        @pl.when(middle)
        def _():
            pass_on(3, 2, dx, down, 4).start()

    lane = lax.broadcasted_iota(jnp.int32, (BLOCK, 128), 1)
    for b in range(REACH, -1, -1):
        doc_in[b].wait()
        cols = jnp.broadcast_to(docs[b], (128, BLOCK)).astype(jnp.float32).T.astype(jnp.int32)
        same = cols == lane
        kv[b * BLOCK:(b + 1) * BLOCK, 0:128] = jnp.where(same, 1.0, 0.0).astype(jnp.bfloat16)
        kv[b * BLOCK:(b + 1) * BLOCK, 384:512] = jnp.ones((BLOCK, 128), jnp.bfloat16)
        if b == REACH:
            tab[...] = jnp.where(same | (lane >= DOCS), 0.0, -PENALTY)

    D = [0, 1, 3, 2]
    own_part(D[0])
    own_part(D[1])
    far_part(D[0])
    near_part(D[0])
    own_part(D[2])
    far_part(D[1])
    near_part(D[1])
    third_part(D[0])
    own_part(D[3])
    far_part(D[2])
    near_part(D[2])
    third_part(D[1])
    far_part(D[3])
    near_part(D[3])
    third_part(D[2])
    third_part(D[3])

    def spread(i, _):
        rows = pl.ds(pl.multiple_of(16 * i, 16), 16)
        ab[rows] = jnp.broadcast_to(tab[rows, :][:, None, :], (16, HEADS, 128)).astype(jnp.bfloat16)
        return 0

    lax.fori_loop(0, BLOCK // 16, spread, 0)

    own_q.wait()
    q_copy(0, 1, came(0, 1)).wait_recv()
    for dx in D:
        arrive(2, dx)

    tiles = CHUNK // TILE
    steps = 4 * tiles

    def place(t):
        order = t // tiles
        dx = order + jnp.where(order == 2, 1, 0) - jnp.where(order == 3, 1, 0)
        chunk = (x - dx + 4) % 4
        return chunk, dx, t % tiles

    def scores(t, slot):
        chunk, _, part = place(t)
        rows = pl.ds(pl.multiple_of(CHUNK * chunk + TILE * part, TILE), TILE)
        left = jnp.concatenate(
            [ab[rows].reshape(ROWS, WIDTH), qb[rows].reshape(ROWS, WIDTH)], axis=1)
        keys = kv[pl.ds(pl.multiple_of(CHUNK * chunk, CHUNK), WINDOW), 0:256]
        sb[slot] = lax.dot_general(
            left, keys, (((1,), (1,)), ((), ())), preferred_element_type=jnp.float32)

    def weigh(t, slot):
        chunk, _, part = place(t)
        token = lax.broadcasted_iota(jnp.int32, (ROWS, CHUNK), 0) // HEADS + TILE * part
        key = lax.broadcasted_iota(jnp.int32, (ROWS, CHUNK), 1)
        last = jnp.where(key <= token, sb[slot, :, WINDOW - CHUNK:], -PENALTY)
        s = jnp.concatenate([sb[slot, :, :WINDOW - CHUNK], last], axis=1)
        top = jnp.max(s, axis=1, keepdims=True)
        weights = jnp.exp2((s - top) * SCALE).astype(jnp.bfloat16)
        vals = kv[pl.ds(pl.multiple_of(CHUNK * chunk, CHUNK), WINDOW), 256:512]
        o = jnp.dot(weights, vals, preferred_element_type=jnp.float32)
        rows = pl.ds(pl.multiple_of(CHUNK * chunk + TILE * part, TILE), TILE)
        ob[rows] = (o[:, :128] / o[:, 128:]).astype(jnp.bfloat16).reshape(TILE, HEADS, WIDTH)

    def pair(j, _):
        t = 2 * j
        scores(t + 1, 1)
        weigh(t, 0)
        following = jnp.minimum(t + 2, steps - 1)

        @pl.when((following % tiles == 0) & (t + 2 < steps))
        def _():
            _, dx, _ = place(following)
            for dc in range(2):
                source = 2 * ((x - dx + 4) % 4) + (core + dc) % 2
                pltpu.make_async_remote_copy(
                    q_hbm.at[:, 0:HEADS, :],
                    qb.at[pl.ds(pl.multiple_of(PIECE * source, PIECE), PIECE)],
                    q_send.at[0], q_recv.at[2 * dx + dc],
                    device_id={"head": source}, device_id_type=MESH).wait_recv()

        scores(following, 0)
        weigh(t + 1, 1)
        return 0

    scores(jnp.int32(0), 0)
    lax.fori_loop(0, steps // 2, pair, 0)
    for dx, dc in PEERS:
        kv_copy(dx, dc, head).wait_send()
        q_copy(dx, dc, head).wait_send()
    for dx in D:
        pass_on(0, 4, dx, (seq + 4) % 32, 0).wait_send()
        pass_on(0, 1, dx, up, 1).wait_send()
        pass_on(0, 3, dx, down, 2).wait_send()

        @pl.when(middle)
        def _():
            pass_on(1, 2, dx, up, 3).wait_send()
            pass_on(3, 2, dx, down, 4).wait_send()


def per_device(queries, keys, values, doc_ids):
    hbm = pl.BlockSpec(memory_space=pltpu.HBM)
    dma = pltpu.SemaphoreType.DMA
    return pl.pallas_call(
        kernel,
        out_shape=jax.ShapeDtypeStruct((BLOCK, HEADS, WIDTH), jnp.bfloat16),
        in_specs=[hbm] * 4,
        out_specs=pl.BlockSpec(memory_space=pltpu.VMEM),
        scratch_shapes=[
            pltpu.VMEM((PIECE, 8, WIDTH), jnp.bfloat16),
            pltpu.VMEM((PIECE, 8, WIDTH), jnp.bfloat16),
            pltpu.VMEM((8, PIECE, 2 * WIDTH), jnp.bfloat16),
            pltpu.VMEM((8, 1, BLOCK), jnp.int32),
            pltpu.VMEM(((REACH + 1) * BLOCK, 512), jnp.bfloat16),
            pltpu.VMEM((BLOCK, HEADS, WIDTH), jnp.bfloat16),
            pltpu.VMEM((BLOCK, HEADS, WIDTH), jnp.bfloat16),
            pltpu.VMEM((BLOCK, 128), jnp.float32),
            pltpu.VMEM((2, ROWS, WINDOW), jnp.float32),
            dma((8,)), dma((8,)), dma((8,)), dma((8,)), dma((20,)), dma((16,)), dma((4,)), dma((5,)),
        ],
        compiler_params=pltpu.CompilerParams(
            collective_id=0, has_side_effects=True, vmem_limit_bytes=30 << 20),
    )(*(pltpu.with_memory_space_constraint(v, pltpu.HBM) for v in (queries, keys, values, doc_ids)))


def solution(mesh):
    spec = P(("seq", "head"), None, None)
    return jax.shard_map(
        per_device, mesh=mesh, in_specs=(spec, spec, spec, P()),
        out_specs=P("seq", "head", None), check_vma=False)
```

```python
import functools
import math

import jax
import jax.numpy as jnp
from jax import lax
from jax.experimental import pallas as pl
from jax.experimental.pallas import tpu as pltpu
from jax.sharding import PartitionSpec as P

MESH = pl.DeviceIdType.MESH
REACH = 4
BLOCK = 512
PIECE = 64
CHUNK = 128
HEADS = 16
WIDTH = 128
WINDOW = REACH * BLOCK + CHUNK
TILE = 32
ROWS = TILE * HEADS
DOCS = 32
PENALTY = 32768.0
SCALE = math.log2(math.e) / math.sqrt(WIDTH)
ORDER = [(0, 0), (0, 1), (1, 0), (3, 0), (1, 1), (3, 1), (2, 0), (2, 1)]
PEERS = ORDER[1:]
PARTS = [0, 1, 3, 2]
EARLY = 8


def kernel(q_hbm, k_hbm, v_hbm, doc_hbm, ob, kin, vin, kvs, docs, kv, qb, ab, tab, sb, acc, tops,
           kv_send, kv_recv, q_send, q_recv, seq_send, seq_recv, loc_sem, doc_sem):
    head, seq = lax.axis_index("head"), lax.axis_index("seq")
    x, core = head // 2, head % 2
    y = seq % 4
    behind = seq >= 4
    middle = (y == 1) | (y == 2)

    def to(dx, dc):
        return 2 * ((x + dx) % 4) + (core + dc) % 2

    def came(dx, dc):
        return 2 * ((x - dx + 4) % 4) + (core + dc) % 2

    k_in = pltpu.make_async_copy(k_hbm, kin, loc_sem.at[2])
    v_in = pltpu.make_async_copy(v_hbm, vin, loc_sem.at[3])
    k_in.start()
    v_in.start()
    doc_in = []
    for b in range(REACH + 1):
        start = pl.multiple_of((seq + 32 - REACH + b) % 32 * BLOCK, BLOCK)
        doc_in.append(pltpu.make_async_copy(doc_hbm.at[pl.ds(start, BLOCK)], docs.at[b, 0], doc_sem.at[b]))
        doc_in[-1].start()
    own_q = pltpu.make_async_copy(
        q_hbm.at[:, pl.ds(pl.multiple_of(HEADS * head, HEADS), HEADS), :],
        qb.at[pl.ds(pl.multiple_of(PIECE * head, PIECE), PIECE)], loc_sem.at[1])
    own_q.start()

    barrier = pltpu.get_barrier_semaphore()
    for dx, dc in PEERS:
        pl.semaphore_signal(barrier, inc=1, device_id={"head": to(dx, dc)}, device_id_type=MESH)
    up = (seq // 4) * 4 + (y + 1) % 4
    down = (seq // 4) * 4 + (y + 3) % 4
    for other in (up, down, (seq + 28) % 32):
        pl.semaphore_signal(barrier, inc=1, device_id={"seq": other}, device_id_type=MESH)

    k_in.wait()
    v_in.wait()
    kvs[:, :, 0:128] = jnp.transpose(kin[...], (1, 0, 2))
    kvs[:, :, 128:256] = jnp.transpose(vin[...], (1, 0, 2))
    pl.semaphore_wait(barrier, len(PEERS) + 3)

    def kv_copy(dx, dc, sender):
        target = to(dx, dc)
        rows = pl.ds(pl.multiple_of(REACH * BLOCK + PIECE * sender, PIECE), PIECE)
        return pltpu.make_async_remote_copy(
            kvs.at[target], kv.at[rows, 128:384],
            kv_send.at[2 * dx + dc], kv_recv.at[2 * dx + dc],
            device_id={"head": target}, device_id_type=MESH)

    def q_copy(dx, dc, sender):
        target = to(dx, dc)
        return pltpu.make_async_remote_copy(
            q_hbm.at[:, pl.ds(pl.multiple_of(HEADS * target, HEADS), HEADS), :],
            qb.at[pl.ds(pl.multiple_of(PIECE * sender, PIECE), PIECE)],
            q_send.at[2 * dx + dc], q_recv.at[2 * dx + dc],
            device_id={"head": target}, device_id_type=MESH)

    own_rows = pl.ds(pl.multiple_of(REACH * BLOCK + PIECE * head, PIECE), PIECE)
    own_kv = pltpu.make_async_copy(kvs.at[head], kv.at[own_rows, 128:384], loc_sem.at[0])
    own_kv.start()
    for dx, dc in PEERS:
        kv_copy(dx, dc, head).start()
    for dx, dc in PEERS:
        q_copy(dx, dc, head).start()

    def part(d, dx):
        slot = REACH if d == 0 else d - 1
        return pl.ds(pl.multiple_of(slot * BLOCK + CHUNK * ((x - dx + 4) % 4), CHUNK), CHUNK)

    def pass_on(src, d, dx, target, lane):
        return pltpu.make_async_remote_copy(
            kv.at[part(src, dx), 128:384], kv.at[part(d, dx), 128:384],
            seq_send.at[4 * lane + dx], seq_recv.at[4 * (d - 1) + dx],
            device_id={"seq": target}, device_id_type=MESH)

    def far_send(dx):
        return pass_on(0, 4, dx, (seq + 4) % 32, 0)

    def arrive(d, dx):
        pass_on(d, d, dx, up, 0).wait_recv()

    def own_part(dx):
        if dx == 0:
            own_kv.wait()
        else:
            kv_copy(dx, 0, came(dx, 0)).wait_recv()
        kv_copy(dx, 1, came(dx, 1)).wait_recv()

        @pl.when(seq < 28)
        def _():
            far_send(dx).start()

        @pl.when(y < 3)
        def _():
            pass_on(0, 1, dx, up, 1).start()

        @pl.when(y == 0)
        def _():
            pass_on(0, 3, dx, down, 2).start()

    def far_part(dx):
        @pl.when(behind)
        def _():
            arrive(4, dx)

        @pl.when(behind & (y > 0))
        def _():
            pass_on(4, 3, dx, down, 2).start()

        @pl.when(behind & (y == 3))
        def _():
            pass_on(4, 1, dx, up, 1).start()

    def near_part(dx):
        @pl.when(behind | (y > 0))
        def _():
            arrive(1, dx)

        @pl.when(middle)
        def _():
            pass_on(1, 2, dx, up, 3).start()

    def third_part(dx):
        @pl.when(behind | (y == 3))
        def _():
            arrive(3, dx)

        @pl.when(behind & middle)
        def _():
            pass_on(3, 2, dx, down, 4).start()

    def second_part(dx):
        @pl.when(behind | (y >= 2))
        def _():
            arrive(2, dx)

    nothing = jnp.zeros((BLOCK, 256), jnp.bfloat16)
    for d in range(1, REACH + 1):
        @pl.when((seq < d))
        def _():
            kv[(d - 1) * BLOCK:d * BLOCK, 128:384] = nothing

    lane = lax.broadcasted_iota(jnp.int32, (BLOCK, 128), 1)
    for d in range(REACH + 1):
        doc_in[REACH - d].wait()
        cols = jnp.broadcast_to(docs[REACH - d], (128, BLOCK)).astype(jnp.float32).T.astype(jnp.int32)
        same = cols == lane
        rows = pl.ds((REACH if d == 0 else d - 1) * BLOCK, BLOCK)
        kv[rows, 0:128] = jnp.where(same, 1.0, 0.0).astype(jnp.bfloat16)
        kv[rows, 384:512] = jnp.ones((BLOCK, 128), jnp.bfloat16)
        if d == 0:
            tab[...] = jnp.where(same | (lane >= DOCS), 0.0, -PENALTY)

    def spread(i, _):
        rows = pl.ds(pl.multiple_of(16 * i, 16), 16)
        ab[rows] = jnp.broadcast_to(tab[rows, :][:, None, :], (16, HEADS, 128)).astype(jnp.bfloat16)
        return 0

    lax.fori_loop(0, BLOCK // 16, spread, 0)

    own_part(PARTS[0])
    own_part(PARTS[1])
    own_part(PARTS[2])
    own_part(PARTS[3])
    far_part(PARTS[0])
    near_part(PARTS[0])
    far_part(PARTS[1])
    near_part(PARTS[1])
    far_part(PARTS[2])
    near_part(PARTS[2])
    far_part(PARTS[3])
    near_part(PARTS[3])
    own_q.wait()

    def piece(t):
        o = t // 2
        dx = jnp.where(o < 2, 0, jnp.where(o >= 6, 2, jnp.where(o % 2 == 0, 1, 3)))
        dc = jnp.where((o == 1) | (o == 4) | (o == 5) | (o == 7), 1, 0)
        return dx, dc, 2 * ((x - dx + 4) % 4) + (core + dc) % 2

    def queries_in(t):
        dx, dc, source = piece(t)
        pltpu.make_async_remote_copy(
            q_hbm.at[:, 0:HEADS, :],
            qb.at[pl.ds(pl.multiple_of(PIECE * source, PIECE), PIECE)],
            q_send.at[0], q_recv.at[2 * dx + dc],
            device_id={"head": source}, device_id_type=MESH).wait_recv()

    def token_rows(t):
        _, _, source = piece(t)
        return pl.ds(pl.multiple_of(PIECE * source + TILE * (t % 2), TILE), TILE)

    def window(t):
        _, _, source = piece(t)
        return pl.ds(pl.multiple_of((REACH - 1) * BLOCK + CHUNK * (source // 2), CHUNK), BLOCK + CHUNK)

    near, far = BLOCK, (REACH - 1) * BLOCK
    total = far + BLOCK + CHUNK

    def scores(kind, t, slot):
        rows = token_rows(t)
        left = jnp.concatenate(
            [ab[rows].reshape(ROWS, WIDTH), qb[rows].reshape(ROWS, WIDTH)], axis=1)

        def dots(keys):
            return lax.dot_general(
                left, keys, (((1,), (1,)), ((), ())), preferred_element_type=jnp.float32)

        lo, hi = {"near": (0, near), "far": (near, far), "all": (0, far)}[kind]
        sb[slot, :, lo:hi] = dots(kv[lo:hi, 0:256])
        if kind != "far":
            sb[slot, :, far:total] = dots(kv[window(t), 0:256])

    def weigh(kind, t, slot):
        lo, hi = {"near": (0, near), "far": (near, far), "all": (0, far)}[kind]
        _, _, source = piece(t)
        if kind == "far":
            s = sb[slot, :, lo:hi]
        else:
            first = PIECE * (source % 2) + TILE * (t % 2)
            token = lax.broadcasted_iota(jnp.int32, (ROWS, CHUNK), 0) // HEADS + first
            key = lax.broadcasted_iota(jnp.int32, (ROWS, CHUNK), 1)
            last = jnp.where(key <= token, sb[slot, :, total - CHUNK:total], -PENALTY)
            s = jnp.concatenate([sb[slot, :, lo:hi], sb[slot, :, far:total - CHUNK], last], axis=1)
        top = jnp.max(s, axis=1, keepdims=True)
        if kind == "far":
            old = tops[t, :, 0:1]
            top = jnp.maximum(top, old)
        weights = jnp.exp2((s - top) * SCALE).astype(jnp.bfloat16)
        o = jnp.dot(weights[:, :hi - lo], kv[lo:hi, 256:512], preferred_element_type=jnp.float32)
        if kind != "far":
            o += jnp.dot(weights[:, hi - lo:], kv[window(t), 256:512], preferred_element_type=jnp.float32)
        if kind == "far":
            o += acc[t] * jnp.exp2((old - top) * SCALE)
        if kind == "near":
            acc[t] = o
            tops[t] = jnp.broadcast_to(top, (ROWS, 128))
        else:
            ob[token_rows(t)] = (o[:, :128] / o[:, 128:]).astype(jnp.bfloat16).reshape(TILE, HEADS, WIDTH)

    def run(kind, begin, end, between, after):
        def pair(j, _):
            t = begin + 2 * j
            scores(kind, t + 1, 1)
            weigh(kind, t, 0)
            between(j)
            scores(kind, t + 2, 0)
            weigh(kind, t + 1, 1)
            return 0

        lax.fori_loop(0, (end - begin) // 2 - 1, pair, 0)
        scores(kind, end - 1, 1)
        weigh(kind, end - 2, 0)
        after()
        weigh(kind, end - 1, 1)

    def near_between(j):
        @pl.when(j < 2)
        def _():
            third_part(jnp.where(j == 0, 0, 3))
            third_part(j + 1)

        queries_in(2 * j + 2)

    def near_after():
        for dx in PARTS:
            second_part(dx)
        scores("far", 0, 0)

    def far_after():
        queries_in(EARLY)
        scores("all", EARLY, 0)

    scores("near", 0, 0)
    run("near", 0, EARLY, near_between, near_after)
    run("far", 0, EARLY, lambda j: None, far_after)
    run("all", EARLY, BLOCK // TILE, lambda j: queries_in(EARLY + 2 * j + 2), lambda: None)

    for dx, dc in PEERS:
        kv_copy(dx, dc, head).wait_send()
        q_copy(dx, dc, head).wait_send()
    for dx in PARTS:
        @pl.when(seq < 28)
        def _():
            far_send(dx).wait_send()

        @pl.when(behind | (y < 3))
        def _():
            pass_on(0, 1, dx, up, 1).wait_send()

        @pl.when(behind | (y == 0))
        def _():
            pass_on(0, 3, dx, down, 2).wait_send()

        @pl.when(middle)
        def _():
            pass_on(1, 2, dx, up, 3).wait_send()

        @pl.when(behind & middle)
        def _():
            pass_on(3, 2, dx, down, 4).wait_send()


def per_device(queries, keys, values, doc_ids):
    hbm = pl.BlockSpec(memory_space=pltpu.HBM)
    dma = pltpu.SemaphoreType.DMA
    return pl.pallas_call(
        kernel,
        out_shape=jax.ShapeDtypeStruct((BLOCK, HEADS, WIDTH), jnp.bfloat16),
        in_specs=[hbm] * 4,
        out_specs=pl.BlockSpec(memory_space=pltpu.VMEM),
        scratch_shapes=[
            pltpu.VMEM((PIECE, 8, WIDTH), jnp.bfloat16),
            pltpu.VMEM((PIECE, 8, WIDTH), jnp.bfloat16),
            pltpu.VMEM((8, PIECE, 2 * WIDTH), jnp.bfloat16),
            pltpu.VMEM((8, 1, BLOCK), jnp.int32),
            pltpu.VMEM(((REACH + 1) * BLOCK, 512), jnp.bfloat16),
            pltpu.VMEM((BLOCK, HEADS, WIDTH), jnp.bfloat16),
            pltpu.VMEM((BLOCK, HEADS, WIDTH), jnp.bfloat16),
            pltpu.VMEM((BLOCK, 128), jnp.float32),
            pltpu.VMEM((2, ROWS, WINDOW), jnp.float32),
            pltpu.VMEM((EARLY, ROWS, 2 * WIDTH), jnp.float32),
            pltpu.VMEM((EARLY, ROWS, 128), jnp.float32),
            dma((8,)), dma((8,)), dma((8,)), dma((8,)), dma((20,)), dma((16,)), dma((4,)), dma((5,)),
        ],
        compiler_params=pltpu.CompilerParams(
            collective_id=0, has_side_effects=True, vmem_limit_bytes=40 << 20),
    )(*(pltpu.with_memory_space_constraint(v, pltpu.HBM) for v in (queries, keys, values, doc_ids)))


def solution(mesh):
    spec = P(("seq", "head"), None, None)
    return jax.shard_map(
        per_device, mesh=mesh, in_specs=(spec, spec, spec, P()),
        out_specs=P("seq", "head", None), check_vma=False)
```

```python
import functools
import math

import jax
import jax.numpy as jnp
from jax import lax
from jax.experimental import pallas as pl
from jax.experimental.pallas import tpu as pltpu
from jax.sharding import PartitionSpec as P

MESH = pl.DeviceIdType.MESH
REACH = 4
BLOCK = 512
PIECE = 64
CHUNK = 128
HEADS = 16
WIDTH = 128
WINDOW = REACH * BLOCK + CHUNK
TILE = 32
ROWS = TILE * HEADS
DOCS = 32
PENALTY = 32768.0
SCALE = math.log2(math.e) / math.sqrt(WIDTH)
ORDER = [(0, 0), (0, 1), (1, 0), (3, 0), (1, 1), (3, 1), (2, 0), (2, 1)]
PEERS = ORDER[1:]
PARTS = [0, 1, 3, 2]
EARLY = 8


def kernel(q_hbm, k_hbm, v_hbm, doc_hbm, ob, kin, vin, kvs, docs, kv, qb, ab, tab, sb, acc, tops,
           kv_send, kv_recv, q_send, q_recv, seq_send, seq_recv, loc_sem, doc_sem):
    head, seq = lax.axis_index("head"), lax.axis_index("seq")
    x, core = head // 2, head % 2
    y = seq % 4
    behind = seq >= 4
    middle = (y == 1) | (y == 2)

    def to(dx, dc):
        return 2 * ((x + dx) % 4) + (core + dc) % 2

    def came(dx, dc):
        return 2 * ((x - dx + 4) % 4) + (core + dc) % 2

    k_in = pltpu.make_async_copy(k_hbm, kin, loc_sem.at[2])
    v_in = pltpu.make_async_copy(v_hbm, vin, loc_sem.at[3])
    k_in.start()
    v_in.start()
    doc_in = []
    for b in range(REACH + 1):
        start = pl.multiple_of((seq + 32 - REACH + b) % 32 * BLOCK, BLOCK)
        doc_in.append(pltpu.make_async_copy(doc_hbm.at[pl.ds(start, BLOCK)], docs.at[b, 0], doc_sem.at[b]))
        doc_in[-1].start()
    own_q = pltpu.make_async_copy(
        q_hbm.at[:, pl.ds(pl.multiple_of(HEADS * head, HEADS), HEADS), :],
        qb.at[pl.ds(pl.multiple_of(PIECE * head, PIECE), PIECE)], loc_sem.at[1])
    own_q.start()

    barrier = pltpu.get_barrier_semaphore()
    for dx, dc in PEERS:
        pl.semaphore_signal(barrier, inc=1, device_id={"head": to(dx, dc)}, device_id_type=MESH)
    up = (seq // 4) * 4 + (y + 1) % 4
    down = (seq // 4) * 4 + (y + 3) % 4
    for other in (up, down, (seq + 28) % 32):
        pl.semaphore_signal(barrier, inc=1, device_id={"seq": other}, device_id_type=MESH)

    k_in.wait()
    v_in.wait()
    kvs[:, :, 0:128] = jnp.transpose(kin[...], (1, 0, 2))
    kvs[:, :, 128:256] = jnp.transpose(vin[...], (1, 0, 2))
    pl.semaphore_wait(barrier, len(PEERS) + 3)

    def kv_copy(dx, dc, sender):
        target = to(dx, dc)
        rows = pl.ds(pl.multiple_of(REACH * BLOCK + PIECE * sender, PIECE), PIECE)
        return pltpu.make_async_remote_copy(
            kvs.at[target], kv.at[rows, 128:384],
            kv_send.at[2 * dx + dc], kv_recv.at[2 * dx + dc],
            device_id={"head": target}, device_id_type=MESH)

    def q_copy(dx, dc, sender):
        target = to(dx, dc)
        return pltpu.make_async_remote_copy(
            q_hbm.at[:, pl.ds(pl.multiple_of(HEADS * target, HEADS), HEADS), :],
            qb.at[pl.ds(pl.multiple_of(PIECE * sender, PIECE), PIECE)],
            q_send.at[2 * dx + dc], q_recv.at[2 * dx + dc],
            device_id={"head": target}, device_id_type=MESH)

    own_rows = pl.ds(pl.multiple_of(REACH * BLOCK + PIECE * head, PIECE), PIECE)
    own_kv = pltpu.make_async_copy(kvs.at[head], kv.at[own_rows, 128:384], loc_sem.at[0])
    own_kv.start()
    for dx, dc in PEERS:
        kv_copy(dx, dc, head).start()
    q_copy(0, 1, head).start()

    def part(d, dx):
        slot = REACH if d == 0 else d - 1
        return pl.ds(pl.multiple_of(slot * BLOCK + CHUNK * ((x - dx + 4) % 4), CHUNK), CHUNK)

    def pass_on(src, d, dx, target, lane):
        return pltpu.make_async_remote_copy(
            kv.at[part(src, dx), 128:384], kv.at[part(d, dx), 128:384],
            seq_send.at[4 * lane + dx], seq_recv.at[4 * (d - 1) + dx],
            device_id={"seq": target}, device_id_type=MESH)

    def far_send(dx):
        return pass_on(0, 4, dx, (seq + 4) % 32, 0)

    def arrive(d, dx):
        pass_on(d, d, dx, up, 0).wait_recv()

    def own_part(dx):
        if dx == 0:
            own_kv.wait()
        else:
            kv_copy(dx, 0, came(dx, 0)).wait_recv()
        kv_copy(dx, 1, came(dx, 1)).wait_recv()

        @pl.when(seq < 28)
        def _():
            far_send(dx).start()

        @pl.when(y < 3)
        def _():
            pass_on(0, 1, dx, up, 1).start()

        @pl.when(y == 0)
        def _():
            pass_on(0, 3, dx, down, 2).start()

    def far_part(dx):
        @pl.when(behind)
        def _():
            arrive(4, dx)

        @pl.when(behind & (y > 0))
        def _():
            pass_on(4, 3, dx, down, 2).start()

        @pl.when(behind & (y == 3))
        def _():
            pass_on(4, 1, dx, up, 1).start()

    def near_part(dx):
        @pl.when(behind | (y > 0))
        def _():
            arrive(1, dx)

        @pl.when(middle)
        def _():
            pass_on(1, 2, dx, up, 3).start()

    def third_part(dx):
        @pl.when(behind | (y == 3))
        def _():
            arrive(3, dx)

        @pl.when(behind & middle)
        def _():
            pass_on(3, 2, dx, down, 4).start()

    def second_part(dx):
        @pl.when(behind | (y >= 2))
        def _():
            arrive(2, dx)

    nothing = jnp.zeros((BLOCK, 256), jnp.bfloat16)
    for d in range(1, REACH + 1):
        @pl.when((seq < d))
        def _():
            kv[(d - 1) * BLOCK:d * BLOCK, 128:384] = nothing

    lane = lax.broadcasted_iota(jnp.int32, (BLOCK, 128), 1)
    for d in range(REACH + 1):
        doc_in[REACH - d].wait()
        cols = jnp.broadcast_to(docs[REACH - d], (128, BLOCK)).astype(jnp.float32).T.astype(jnp.int32)
        same = cols == lane
        rows = pl.ds((REACH if d == 0 else d - 1) * BLOCK, BLOCK)
        kv[rows, 0:128] = jnp.where(same, 1.0, 0.0).astype(jnp.bfloat16)
        kv[rows, 384:512] = jnp.ones((BLOCK, 128), jnp.bfloat16)
        if d == 0:
            tab[...] = jnp.where(same | (lane >= DOCS), 0.0, -PENALTY)

    def spread(i, _):
        rows = pl.ds(pl.multiple_of(16 * i, 16), 16)
        ab[rows] = jnp.broadcast_to(tab[rows, :][:, None, :], (16, HEADS, 128)).astype(jnp.bfloat16)
        return 0

    lax.fori_loop(0, BLOCK // 16, spread, 0)

    own_part(PARTS[0])
    own_part(PARTS[1])
    own_part(PARTS[2])
    own_part(PARTS[3])
    for dx, dc in PEERS[1:]:
        q_copy(dx, dc, head).start()
    far_part(PARTS[0])
    near_part(PARTS[0])
    far_part(PARTS[1])
    near_part(PARTS[1])
    far_part(PARTS[2])
    near_part(PARTS[2])
    far_part(PARTS[3])
    near_part(PARTS[3])
    own_q.wait()

    def piece(t):
        o = t // 2
        dx = jnp.where(o < 2, 0, jnp.where(o >= 6, 2, jnp.where(o % 2 == 0, 1, 3)))
        dc = jnp.where((o == 1) | (o == 4) | (o == 5) | (o == 7), 1, 0)
        return dx, dc, 2 * ((x - dx + 4) % 4) + (core + dc) % 2

    def queries_in(t):
        dx, dc, source = piece(t)
        pltpu.make_async_remote_copy(
            q_hbm.at[:, 0:HEADS, :],
            qb.at[pl.ds(pl.multiple_of(PIECE * source, PIECE), PIECE)],
            q_send.at[0], q_recv.at[2 * dx + dc],
            device_id={"head": source}, device_id_type=MESH).wait_recv()

    def token_rows(t):
        _, _, source = piece(t)
        return pl.ds(pl.multiple_of(PIECE * source + TILE * (t % 2), TILE), TILE)

    def window(t):
        _, _, source = piece(t)
        return pl.ds(pl.multiple_of((REACH - 1) * BLOCK + CHUNK * (source // 2), CHUNK), BLOCK + CHUNK)

    near, far = BLOCK, (REACH - 1) * BLOCK
    total = far + BLOCK + CHUNK

    def scores(kind, t, slot):
        rows = token_rows(t)
        left = jnp.concatenate(
            [ab[rows].reshape(ROWS, WIDTH), qb[rows].reshape(ROWS, WIDTH)], axis=1)

        def dots(keys):
            return lax.dot_general(
                left, keys, (((1,), (1,)), ((), ())), preferred_element_type=jnp.float32)

        lo, hi = {"near": (0, near), "far": (near, far), "all": (0, far)}[kind]
        sb[slot, :, lo:hi] = dots(kv[lo:hi, 0:256])
        if kind != "far":
            sb[slot, :, far:total] = dots(kv[window(t), 0:256])

    def weigh(kind, t, slot):
        lo, hi = {"near": (0, near), "far": (near, far), "all": (0, far)}[kind]
        _, _, source = piece(t)
        if kind == "far":
            s = sb[slot, :, lo:hi]
        else:
            first = PIECE * (source % 2) + TILE * (t % 2)
            token = lax.broadcasted_iota(jnp.int32, (ROWS, CHUNK), 0) // HEADS + first
            key = lax.broadcasted_iota(jnp.int32, (ROWS, CHUNK), 1)
            last = jnp.where(key <= token, sb[slot, :, total - CHUNK:total], -PENALTY)
            s = jnp.concatenate([sb[slot, :, lo:hi], sb[slot, :, far:total - CHUNK], last], axis=1)
        top = jnp.max(s, axis=1, keepdims=True)
        if kind == "far":
            old = tops[t, :, 0:1]
            top = jnp.maximum(top, old)
        weights = jnp.exp2((s - top) * SCALE).astype(jnp.bfloat16)
        o = jnp.dot(weights[:, :hi - lo], kv[lo:hi, 256:512], preferred_element_type=jnp.float32)
        if kind != "far":
            o += jnp.dot(weights[:, hi - lo:], kv[window(t), 256:512], preferred_element_type=jnp.float32)
        if kind == "far":
            o += acc[t] * jnp.exp2((old - top) * SCALE)
        if kind == "near":
            acc[t] = o
            tops[t] = jnp.broadcast_to(top, (ROWS, 128))
        else:
            ob[token_rows(t)] = (o[:, :128] / o[:, 128:]).astype(jnp.bfloat16).reshape(TILE, HEADS, WIDTH)

    def run(kind, begin, end, between, after):
        def pair(j, _):
            t = begin + 2 * j
            scores(kind, t + 1, 1)
            weigh(kind, t, 0)
            between(j)
            scores(kind, t + 2, 0)
            weigh(kind, t + 1, 1)
            return 0

        lax.fori_loop(0, (end - begin) // 2 - 1, pair, 0)
        scores(kind, end - 1, 1)
        weigh(kind, end - 2, 0)
        after()
        weigh(kind, end - 1, 1)

    def near_between(j):
        @pl.when(j < 2)
        def _():
            third_part(jnp.where(j == 0, 0, 3))
            third_part(j + 1)

        queries_in(2 * j + 2)

    def near_after():
        for dx in PARTS:
            second_part(dx)
        scores("far", 0, 0)

    def far_after():
        queries_in(EARLY)
        scores("all", EARLY, 0)

    scores("near", 0, 0)
    run("near", 0, EARLY, near_between, near_after)
    run("far", 0, EARLY, lambda j: None, far_after)
    run("all", EARLY, BLOCK // TILE, lambda j: queries_in(EARLY + 2 * j + 2), lambda: None)

    for dx, dc in PEERS:
        kv_copy(dx, dc, head).wait_send()
        q_copy(dx, dc, head).wait_send()
    for dx in PARTS:
        @pl.when(seq < 28)
        def _():
            far_send(dx).wait_send()

        @pl.when(behind | (y < 3))
        def _():
            pass_on(0, 1, dx, up, 1).wait_send()

        @pl.when(behind | (y == 0))
        def _():
            pass_on(0, 3, dx, down, 2).wait_send()

        @pl.when(middle)
        def _():
            pass_on(1, 2, dx, up, 3).wait_send()

        @pl.when(behind & middle)
        def _():
            pass_on(3, 2, dx, down, 4).wait_send()


def per_device(queries, keys, values, doc_ids):
    hbm = pl.BlockSpec(memory_space=pltpu.HBM)
    dma = pltpu.SemaphoreType.DMA
    return pl.pallas_call(
        kernel,
        out_shape=jax.ShapeDtypeStruct((BLOCK, HEADS, WIDTH), jnp.bfloat16),
        in_specs=[hbm] * 4,
        out_specs=pl.BlockSpec(memory_space=pltpu.VMEM),
        scratch_shapes=[
            pltpu.VMEM((PIECE, 8, WIDTH), jnp.bfloat16),
            pltpu.VMEM((PIECE, 8, WIDTH), jnp.bfloat16),
            pltpu.VMEM((8, PIECE, 2 * WIDTH), jnp.bfloat16),
            pltpu.VMEM((8, 1, BLOCK), jnp.int32),
            pltpu.VMEM(((REACH + 1) * BLOCK, 512), jnp.bfloat16),
            pltpu.VMEM((BLOCK, HEADS, WIDTH), jnp.bfloat16),
            pltpu.VMEM((BLOCK, HEADS, WIDTH), jnp.bfloat16),
            pltpu.VMEM((BLOCK, 128), jnp.float32),
            pltpu.VMEM((2, ROWS, WINDOW), jnp.float32),
            pltpu.VMEM((EARLY, ROWS, 2 * WIDTH), jnp.float32),
            pltpu.VMEM((EARLY, ROWS, 128), jnp.float32),
            dma((8,)), dma((8,)), dma((8,)), dma((8,)), dma((20,)), dma((16,)), dma((4,)), dma((5,)),
        ],
        compiler_params=pltpu.CompilerParams(
            collective_id=0, has_side_effects=True, vmem_limit_bytes=40 << 20),
    )(*(pltpu.with_memory_space_constraint(v, pltpu.HBM) for v in (queries, keys, values, doc_ids)))


def solution(mesh):
    spec = P(("seq", "head"), None, None)
    return jax.shard_map(
        per_device, mesh=mesh, in_specs=(spec, spec, spec, P()),
        out_specs=P("seq", "head", None), check_vma=False)
```
